32 devices in a mesh: ctx: 8 (over z, y), exp: 4 (over x, core).
Axes of the slice: x: 2, y: 2, z: 4, core: 2. Of those that a mesh axis runs over, the one named last changes fastest.
Arguments:
- residual: bfloat16 [1024, 6144], P('ctx', 'exp'), may hold values from -6 to 6
- query_rows: bfloat16 [1024, 6144], P('ctx', 'exp'), may hold values from -2 to 2
- key_rows: bfloat16 [1024, 6144], P('ctx', 'exp'), may hold values from -2 to 2
- value_rows: bfloat16 [1024, 6144], P('ctx', 'exp'), may hold values from -6 to 6
- log_decay: float32 [1024, 48], P('ctx', 'exp'), may hold values from -1 to 0
- norm_gain: bfloat16 [6144], P('exp'), may hold values from 0.5 to 1.5
- expert_ids: int32 [1024, 2], P('ctx'), may hold values from 0 to 3, all different within a row; in each aligned block of 128 rows (0 to 127, 128 to 255, ...) at most 96 rows name the same one
- gate_weights: float32 [1024, 2], P('ctx'), may hold values from 0.2 to 1
- w_gate: bfloat16 [4, 6144, 9216], P('exp', None, 'ctx'), may hold values from -0.078125 to 0.078125
- w_up: bfloat16 [4, 6144, 9216], P('exp', None, 'ctx'), may hold values from -0.078125 to 0.078125
- w_down: bfloat16 [4, 9216, 6144], P('exp', 'ctx'), may hold values from -0.0625 to 0.0625
Outputs:
- mixed: bfloat16 [1024, 6144], P('ctx', 'exp')
The draws below stay inside these ranges and needn't reach their ends.
Inputs may be any that keep to these rules, and one draw needn't show every extreme that they name: `expert_ids`: each token names two different experts; among the 128 tokens of one block at most 96 name any one expert, and in every draw some expert is named by exactly 96 tokens of some block.
All inputs are finite; a program needn't handle non-finite values.
Results may differ from the reference program's by a relative error of at most 0.015.
Values may be sent and summed in bfloat16 or wider, within the bound.
No kernel may reach another device: no remote copies, remote signals or barrier semaphores. Data moves between devices by JAX's collectives and lax.ppermute only.
A program may use at most 128 MiB of HBM per device.

```python
import math
import jax
import jax.numpy as jnp
import numpy as np
from jax import lax

D = 6144
FF = 9216
HEAD = 128
TOK = 128
CONTEXT_LENGTH = 1024
HEADS = 48
EXPERTS = 4
CAP = 96
N_CTX = 8


def draw_log_decay(key, part):
    stochastic_seeds = jax.random.split(key, 5)
    slow_share = 0.5
    slow_heads = jax.random.uniform(stochastic_seeds[0], (HEADS,)) < slow_share
    forgetting_speeds = jnp.where(slow_heads, 0.5 / CONTEXT_LENGTH, 1.0 / 40.0)
    jitter_bias = jnp.exp(jax.random.uniform(stochastic_seeds[1], (CONTEXT_LENGTH, HEADS), minval=-0.69, maxval=0.69))
    magnitude_for_chip_share = jnp.exp(jax.random.uniform(stochastic_seeds[2], (CONTEXT_LENGTH // TOK, 1, HEADS), minval=-0.69, maxval=0.69))
    magnitude_for_chip_share = jnp.broadcast_to(magnitude_for_chip_share, (CONTEXT_LENGTH // TOK, TOK, HEADS)).reshape(CONTEXT_LENGTH, HEADS)
    packet_batches = jax.random.uniform(stochastic_seeds[3], (CONTEXT_LENGTH, 1)) < 4.0 / CONTEXT_LENGTH
    objective_terms = jnp.log(jax.random.uniform(stochastic_seeds[4], (CONTEXT_LENGTH, 1), minval=0.5, maxval=0.8))
    layer_answer = -forgetting_speeds[None, :] * jitter_bias * magnitude_for_chip_share + jnp.where(packet_batches, objective_terms, 0.0)
    return layer_answer.astype(jnp.float32)


def steps_of(key, dims, shards, smallest, top_value):
    level = 1.0
    for dim, parts in shards:
        draws = jax.random.uniform(jax.random.fold_in(jax.random.fold_in(key, 6), dim), (parts,), jnp.float32, smallest / len(shards), top_value / len(shards))
        level = level * jnp.repeat(jnp.exp(draws), dims[dim] // parts).reshape((-1,) + (1,) * (len(dims) - 1 - dim))
    return level


def shared_out(own_key, own, number, rows, amount, top, limit, skew):
    ranking = jax.random.permutation(own_key, amount)
    heavy_load, common = portions_of(amount, rows * top, limit, skew, True), portions_of(amount, rows * top, limit, skew, False)
    places = jnp.arange(amount)

    def named(sizes, offset_by):
        used = int((sizes > 0).sum())
        fixed = max(1, used // 4)
        moved = fixed + (places - fixed + offset_by * (used - fixed)) % max(1, amount - fixed)
        return jnp.zeros((amount,), jnp.int32).at[ranking[jnp.where(places < fixed, places, moved)]].set(jnp.asarray(sizes, jnp.int32))

    sizes = jnp.where(number % 4 == 0, named(heavy_load, number // 4), named(common, number - number // 4 - 1))
    mixed = jax.random.permutation(jax.random.fold_in(own, 3), amount)
    donor, taker = mixed[0:amount // 2 * 2:2], mixed[1:amount // 2 * 2:2]
    room = jnp.minimum(sizes[donor] - 1, limit - sizes[taker]) // 2
    room = jnp.where((donor == ranking[0]) | (taker == ranking[0]) | (sizes[taker] == 0), 0, jnp.maximum(room, 0))
    moved = jax.random.randint(jax.random.fold_in(own, 4), (amount // 2,), 0, 1 << 20) % (room + 1)
    sizes = sizes.at[donor].add(-moved).at[taker].add(moved)
    members = jnp.searchsorted(jnp.cumsum(sizes), jnp.arange(rows * top), side="right").astype(jnp.int32)
    grid = members.reshape(top, rows).T
    grid = grid[jax.random.permutation(jax.random.fold_in(own, 1), rows)]
    offset_by = jax.random.randint(jax.random.fold_in(own, 2), (rows, 1), 0, top)
    return jnp.take_along_axis(grid, (jnp.arange(top)[None, :] + offset_by) % top, axis=1)


def portions_of(amount, total, limit, skew, full):
    loads = [(1 << 20) // math.isqrt(grade ** skew) + 1 for grade in range(1, amount + 1)]
    largest = limit if full else min(limit, max(-(-total // amount), total * loads[0] // sum(loads)))
    least = 1 if total - largest >= amount - 1 else 0
    counts, spare = [largest] + [least] * (amount - 1), total - largest - least * (amount - 1)
    while spare > 0:
        movable = [i for i in range(1, amount) if counts[i] < largest] or [i for i in range(1, amount) if counts[i] < limit]
        whole, remaining = sum([loads[i] for i in movable]), spare
        for i in movable:
            addition = min(limit - counts[i], max(1, remaining * loads[i] // whole), spare)
            counts[i] = counts[i] + addition
            spare = spare - addition
    return np.array(counts)


def noise(key, extent, scale, limit, shards=(), held_as=jnp.bfloat16):
    entries = jax.random.normal(key, extent, jnp.float32) * scale
    if len(shards) > 0:
        entries = steps_of(key, extent, shards, -0.22, 0.18) * entries
    return jnp.clip(entries, min=-limit, max=limit).astype(held_as)


def setup_inputs(seed: int = 0) -> dict:
    key_list = jax.random.split(jax.random.key(seed), 12)
    residual = noise(key_list[0], (CONTEXT_LENGTH, D), 1.0, 6.0, ((0, 8), (1, 4)))
    query_rows = noise(key_list[1], (CONTEXT_LENGTH, D), 0.3, 2.0, ((0, 8), (1, 4)))
    key_rows = noise(key_list[2], (CONTEXT_LENGTH, D), 0.3, 2.0, ((0, 8), (1, 4)))
    value_rows = noise(key_list[3], (CONTEXT_LENGTH, D), 1.0, 6.0, ((0, 8), (1, 4)))
    log_decay = draw_log_decay(jax.random.fold_in(key_list[11], 71), 0)
    norm_gain = jnp.clip(1.0 + 0.1 * jax.random.normal(key_list[5], (D,), jnp.float32), 0.5, 1.5).astype(jnp.bfloat16)
    expert_ids_keys = jax.random.split(jax.random.fold_in(key_list[6], 1), CONTEXT_LENGTH // TOK)
    expert_ids_turns = jax.random.permutation(jax.random.fold_in(key_list[6], 3), CONTEXT_LENGTH // TOK)
    expert_ids = jax.vmap(lambda own, number: shared_out(jax.random.fold_in(key_list[6], 2), own, number, TOK, EXPERTS, 2, CAP, 2))(expert_ids_keys, expert_ids_turns).reshape((CONTEXT_LENGTH, 2))
    gate_weights = jnp.clip(0.2 + 0.8 * jax.random.uniform(key_list[7], (CONTEXT_LENGTH, 2), jnp.float32) ** steps_of(key_list[7], (CONTEXT_LENGTH, 2), ((0, 8),), -0.2, 0.2), 0.2, 1.0)
    w_gate = noise(key_list[8], (EXPERTS, D, FF), D ** -0.5, 0.078125, ((0, 4), (2, 8)))
    w_up = noise(key_list[9], (EXPERTS, D, FF), D ** -0.5, 0.078125, ((0, 4), (2, 8)))
    w_down = noise(key_list[10], (EXPERTS, FF, D), FF ** -0.5, 0.0625, ((0, 4), (1, 8)))
    return dict(residual=residual, query_rows=query_rows, key_rows=key_rows, value_rows=value_rows, log_decay=log_decay, norm_gain=norm_gain, expert_ids=expert_ids, gate_weights=gate_weights, w_gate=w_gate, w_up=w_up, w_down=w_down)


precise = lax.Precision.HIGHEST

def matmul(left, right):
    return jnp.dot(left, right, preferred_element_type=jnp.float32)

def span_parts(query_blk, key_blk, value_blk, decay_blk):
    cumul = jnp.cumsum(decay_blk, axis=0)
    length = decay_blk.shape[0]
    causal = (jnp.arange(length)[:, None] >= jnp.arange(length)[None, :])[:, :, None]
    spread = cumul[:, None, :] - cumul[None, :, :]
    fading = jnp.where(causal, jnp.exp(jnp.where(causal, spread, 0.0)), 0.0)
    query_f = query_blk.astype(jnp.float32)
    key_f = key_blk.astype(jnp.float32)
    value_f = value_blk.astype(jnp.float32)
    scores = jnp.einsum('thd,uhd->htu', query_f, key_f) * jnp.transpose(fading, (2, 0, 1))
    scores = lax.optimization_barrier(scores.astype(jnp.bfloat16))
    inside = jnp.einsum('htu,uhd->thd', scores.astype(jnp.float32), value_f)
    tail = jnp.exp(cumul[-1][None, :] - cumul)
    local = jnp.einsum('uhd,uhe->hde', key_f * tail[:, :, None], value_f, precision=precise)
    return (inside, cumul, query_f, jnp.exp(cumul[-1]), local)

def head_norm(attended, gain):
    meansq = lax.optimization_barrier(jnp.mean(attended * attended, axis=-1, keepdims=True))
    return attended * lax.rsqrt(meansq + 1e-05) * gain

def reference(residual, query_rows, key_rows, value_rows, log_decay, norm_gain, expert_ids, gate_weights, w_gate, w_up, w_down):
    heads = D // HEAD
    shaped = (N_CTX, TOK, heads, HEAD)

    def advance(state, block):
        query_blk, key_blk, value_blk, decay_blk = block
        inside, cumul, query_f, factor, local = span_parts(query_blk, key_blk, value_blk, decay_blk)
        carried = jnp.exp(cumul)[:, :, None] * jnp.einsum('thd,hde->the', query_f, state, precision=precise)
        return (factor[:, None, None] * state + local, inside + carried)
    start_state = jnp.zeros((heads, HEAD, HEAD), jnp.float32)
    _, outputs = lax.scan(advance, start_state, (query_rows.reshape(shaped), key_rows.reshape(shaped), value_rows.reshape(shaped), log_decay.reshape(N_CTX, TOK, heads)))
    attended = outputs.reshape(CONTEXT_LENGTH, heads, HEAD)
    normed = head_norm(attended, norm_gain.astype(jnp.float32).reshape(heads, HEAD)).reshape(CONTEXT_LENGTH, D)
    hidden = (residual.astype(jnp.float32) + normed).astype(jnp.bfloat16)
    flat_ids = expert_ids.reshape(N_CTX, 2 * TOK)
    onehot = (flat_ids[:, :, None] == jnp.arange(EXPERTS, dtype=jnp.int32)[None, None, :]).astype(jnp.int32)
    earlier = jnp.cumsum(onehot, axis=1) - onehot
    slots = lax.optimization_barrier(jnp.sum(earlier * onehot, axis=2)).astype(jnp.int32)
    places = (flat_ids * CAP + slots).astype(jnp.int32)
    select = (jnp.arange(EXPERTS * CAP, dtype=jnp.int32)[None, :, None] == places[:, None, :]).astype(jnp.float32)
    select = select.reshape(N_CTX, EXPERTS * CAP, TOK, 2).sum(axis=3)
    hidden_blk = hidden.reshape(N_CTX, TOK, D).astype(jnp.float32)
    buckets = jnp.einsum('cst,ctd->csd', select, hidden_blk).astype(jnp.bfloat16)
    per_expert = buckets.reshape(N_CTX, EXPERTS, CAP, D).transpose(1, 0, 2, 3).reshape(EXPERTS, N_CTX * CAP, D)

    def run_expert(operands):
        rows_in, gate_w, up_w, down_w = operands
        act = (jax.nn.silu(matmul(rows_in, gate_w)) * matmul(rows_in, up_w)).astype(jnp.bfloat16)
        act_parts = act.reshape(N_CTX * CAP, N_CTX, FF // N_CTX).transpose(1, 0, 2)
        down_parts = down_w.reshape(N_CTX, FF // N_CTX, D)

        def accumulate(total, piece):
            part_act, part_down = piece
            term = lax.optimization_barrier(matmul(part_act, part_down).astype(jnp.bfloat16))
            return (total + term.astype(jnp.float32), None)
        total, _ = lax.scan(accumulate, jnp.zeros((N_CTX * CAP, D), jnp.float32), (act_parts, down_parts))
        return total.astype(jnp.bfloat16)
    expert_out = lax.map(run_expert, (per_expert, w_gate, w_up, w_down))
    back = expert_out.reshape(EXPERTS, N_CTX, CAP, D).transpose(1, 0, 2, 3).reshape(N_CTX, EXPERTS * CAP, D)
    picked = jax.vmap(lambda table, where_at: jnp.take(table, where_at, axis=0))(back, places)
    picked = picked.astype(jnp.float32).reshape(N_CTX, TOK, 2, D)
    mixed = hidden_blk + lax.optimization_barrier(jnp.sum(gate_weights.reshape(N_CTX, TOK, 2, 1) * picked, axis=2))
    return mixed.reshape(CONTEXT_LENGTH, D).astype(jnp.bfloat16)
```

```python
import functools

import jax
import jax.numpy as jnp
from jax import lax
from jax.experimental import pallas as pl
from jax.experimental.pallas import tpu as pltpu
from jax.sharding import PartitionSpec as P

HEAD = 128
VMEM_LIMIT = 60 * 1024 * 1024

precise = lax.Precision.HIGHEST
f32 = jnp.float32
bf16 = jnp.bfloat16


def swap(value, bit):
    axis, mask = bit
    return lax.ppermute(value, axis, [(i, i ^ mask) for i in range(lax.axis_size(axis))])


def is_set(bit, ctx_rel, exp_rel):
    axis, mask = bit
    return 1 if ((ctx_rel if axis == "ctx" else exp_rel) & mask) else 0


def position(axes, ctx_rel, exp_rel):
    return tuple(is_set(bit, ctx_rel, exp_rel) for bit in axes)


def local_kernel(heads, per, q_ref, k_ref, v_ref, decay_ref, inside_ref, cumul_ref, local_ref, *sends):
    count = q_ref.shape[0]
    rows = lax.broadcasted_iota(jnp.int32, (count, count), 0)
    cols = lax.broadcasted_iota(jnp.int32, (count, count), 1)
    causal = rows >= cols
    decay = decay_ref[...]
    cumul = jnp.dot(causal.astype(f32), decay, precision=precise, preferred_element_type=f32)
    across = lax.dot_general(
        decay, (rows <= cols).astype(f32), (((0,), (0,)), ((), ())),
        precision=precise, preferred_element_type=f32,
    )
    cumul_ref[...] = cumul
    for h in range(heads):
        span = slice(h * HEAD, (h + 1) * HEAD)
        query, key, value = q_ref[:, span], k_ref[:, span], v_ref[:, span]
        col, row = cumul[:, h : h + 1], across[h : h + 1, :]
        fading = jnp.where(causal, jnp.exp(jnp.where(causal, col - row, 0.0)), 0.0)
        dots = lax.dot_general(query, key, (((1,), (1,)), ((), ())), preferred_element_type=f32)
        scores = (dots * fading).astype(bf16)
        inside_ref[:, span] = jnp.dot(scores, value, preferred_element_type=f32)
        tail = jnp.exp(col[count - 1 :, :] - col)
        faded = key.astype(f32) * tail
        high = faded.astype(bf16)
        low = (faded - high.astype(f32)).astype(bf16)
        turned = (((0,), (0,)), ((), ()))
        state = lax.dot_general(high, value, turned, preferred_element_type=f32)
        state = state + lax.dot_general(low, value, turned, preferred_element_type=f32)
        local_ref[h] = state
        sends[h // per][h % per] = state.astype(bf16)


def local_parts(query, key, value, decay, per):
    count, columns = query.shape
    heads = columns // HEAD
    chunks = heads // per
    return pl.pallas_call(
        functools.partial(local_kernel, heads, per),
        out_shape=[
            jax.ShapeDtypeStruct((count, columns), f32),
            jax.ShapeDtypeStruct((count, heads), f32),
            jax.ShapeDtypeStruct((heads, HEAD, HEAD), f32),
        ]
        + [jax.ShapeDtypeStruct((per, HEAD, HEAD), bf16)] * chunks,
        compiler_params=pltpu.CompilerParams(vmem_limit_bytes=VMEM_LIMIT),
        name="local_parts",
    )(query, key, value, decay)


def hidden_kernel(first, per, q_ref, inside_ref, residual_ref, gain_ref, cumul_ref, state_ref, out_ref):
    for i in range(per):
        span = slice(i * HEAD, (i + 1) * HEAD)
        grown = jnp.exp(cumul_ref[:, first + i : first + i + 1])
        carried = jnp.dot(q_ref[:, span], state_ref[i], preferred_element_type=f32)
        attended = inside_ref[:, span] + grown * carried
        meansq = jnp.mean(attended * attended, axis=-1, keepdims=True)
        normed = attended * lax.rsqrt(meansq + 1e-05) * gain_ref[:, span].astype(f32)
        out_ref[:, span] = (residual_ref[:, span].astype(f32) + normed).astype(bf16)


def hidden_rows(chunk, per, query, inside, residual, gain, cumul, state):
    count = query.shape[0]
    width = per * HEAD
    here = lambda i: (0, chunk)
    return pl.pallas_call(
        functools.partial(hidden_kernel, chunk * per, per),
        grid=(1,),
        in_specs=[
            pl.BlockSpec((count, width), here),
            pl.BlockSpec((count, width), here),
            pl.BlockSpec((count, width), here),
            pl.BlockSpec((1, width), here),
            pl.BlockSpec(cumul.shape, lambda i: (0, 0)),
            pl.BlockSpec(state.shape, lambda i: (0, 0, 0)),
        ],
        out_specs=pl.BlockSpec((count, width), lambda i: (0, 0)),
        out_shape=jax.ShapeDtypeStruct((count, width), bf16),
        name=f"hidden_rows_{chunk}",
    )(query, inside, residual, gain, cumul, state)


def expert_in_kernel(plan, has_sum, last, idx_ref, *refs):
    del idx_ref
    pieces, axes, last_bit, core_bit, ctx_size, exp_size, group = plan
    arrays, refs = refs[:pieces], refs[pieces:]
    gates, refs = refs[:exp_size], refs[exp_size:]
    ups, refs = refs[:exp_size], refs[exp_size:]
    sum_ref, refs = (refs[0], refs[1:]) if has_sum else (None, refs)
    scale_ref, refs = (refs[0], refs[1:]) if last else (None, refs)
    out_ref = refs[0]
    count = arrays[0].shape[-2]
    tile = gates[0].shape[1]
    if last:
        eye = (
            lax.broadcasted_iota(jnp.int32, (count, count), 0)
            == lax.broadcasted_iota(jnp.int32, (count, count), 1)
        ).astype(f32)
        scales = lax.dot_general(
            eye, scale_ref[...], (((1,), (1,)), ((), ())), precision=precise, preferred_element_type=f32
        )
    for start in range(0, ctx_size, group):
        blocks = range(start, start + group)
        rows = slice(start * count, (start + group) * count)
        total = sum_ref[0, rows, :] if has_sum else None
        for r in range(exp_size):
            parts = []
            for i in blocks:
                ref = arrays[2 * is_set(last_bit, i, r) + is_set(core_bit, i, r)]
                parts.append(ref[position(axes, i, r)])
            piece = jnp.concatenate(parts, axis=0)
            weights = jnp.concatenate([gates[r][...], ups[r][...]], axis=1)
            term = jnp.dot(piece, weights, preferred_element_type=f32)
            total = term if total is None else total + term
        if last:
            gate, up = total[:, :tile], total[:, tile:]
            act = gate / (1.0 + jnp.exp(-gate)) * up
            for i in blocks:
                local = slice((i - start) * count, (i - start + 1) * count)
                out_ref[i * count : (i + 1) * count, :] = (act[local] * scales[:, i : i + 1]).astype(bf16)
        else:
            out_ref[0, rows, :] = total


def expert_in(arrays, axes, last_bit, core_bit, idx, w_gate, w_up, total, scale, ctx_size, exp_size):
    count, width = arrays[0].shape[-2:]
    units = w_gate.shape[1]
    tile = 384 if units % 384 == 0 else units
    tiles = units // tile
    has_sum, last = total is not None, scale is not None
    group = min(4, ctx_size)
    plan = (len(arrays), axes, last_bit, core_bit, ctx_size, exp_size, group)
    rows = ctx_size * count
    in_specs = [
        pl.BlockSpec(a.shape, (lambda n, idx, d=a.ndim: (0,) * d), pipeline_mode=pl.Buffered(1)) for a in arrays
    ]
    weight_specs = [pl.BlockSpec((width, tile), lambda n, idx, r=r: (idx[r], n)) for r in range(exp_size)]
    in_specs += weight_specs + weight_specs
    operands = list(arrays) + [w_gate] * exp_size + [w_up] * exp_size
    sum_spec = pl.BlockSpec((1, rows, 2 * tile), lambda n, idx: (n, 0, 0))
    aliases = {}
    if has_sum:
        in_specs.append(sum_spec)
        operands.append(total)
        if not last:
            aliases = {len(operands): 0}
    if last:
        in_specs.append(pl.BlockSpec(scale.shape, lambda n, idx: (0, 0)))
        operands.append(scale)
        out_spec = pl.BlockSpec((rows, tile), lambda n, idx: (0, n))
        out_shape = jax.ShapeDtypeStruct((rows, units), bf16)
    else:
        out_spec = sum_spec
        out_shape = jax.ShapeDtypeStruct((tiles, rows, 2 * tile), f32)
    flops = 4 * rows * width * exp_size * units
    return pl.pallas_call(
        functools.partial(expert_in_kernel, plan, has_sum, last),
        grid_spec=pltpu.PrefetchScalarGridSpec(
            num_scalar_prefetch=1, grid=(tiles,), in_specs=in_specs, out_specs=out_spec
        ),
        out_shape=out_shape,
        input_output_aliases=aliases,
        cost_estimate=pl.CostEstimate(
            flops=flops, transcendentals=0, bytes_accessed=4 * exp_size * width * units + 8 * rows * units
        ),
        compiler_params=pltpu.CompilerParams(vmem_limit_bytes=VMEM_LIMIT),
        name="expert_in_last" if last else "expert_in",
    )(idx, *operands)


def expert_out_kernel(plan, idx_ref, act_ref, w_ref, *outs):
    del idx_ref
    axes, first_bit, core_bit, ctx_size, order, group = plan
    count = outs[0].shape[-2]
    step = pl.program_id(0)
    for s, r in enumerate(order):

        @pl.when(step == s)
        def _(r=r):
            for start in range(0, ctx_size, group):
                rows = slice(start * count, (start + group) * count)
                term = jnp.dot(act_ref[rows, :], w_ref[...], preferred_element_type=f32).astype(bf16)
                for i in range(start, start + group):
                    ref = outs[2 * is_set(core_bit, i, r) + is_set(first_bit, i, r)]
                    ref[position(axes, i, r)] = term[(i - start) * count : (i - start + 1) * count]


def expert_out(act, w_down, idx, order, axes, first_bit, core_bit, ctx_size, width):
    rows, units = act.shape
    count = rows // ctx_size
    exp_size = len(order)
    plan = (axes, first_bit, core_bit, ctx_size, order, min(4, ctx_size))
    shape = (2,) * len(axes) + (count, width)
    return pl.pallas_call(
        functools.partial(expert_out_kernel, plan),
        grid_spec=pltpu.PrefetchScalarGridSpec(
            num_scalar_prefetch=1,
            grid=(exp_size,),
            in_specs=[
                pl.BlockSpec(act.shape, lambda s, idx: (0, 0), pipeline_mode=pl.Buffered(1)),
                pl.BlockSpec((units, width), lambda s, idx: (0, idx[s])),
            ],
            out_specs=[pl.BlockSpec(shape, lambda s, idx: (0,) * len(shape))] * 4,
        ),
        out_shape=[jax.ShapeDtypeStruct(shape, bf16)] * 4,
        cost_estimate=pl.CostEstimate(
            flops=2 * rows * units * width * exp_size,
            transcendentals=0,
            bytes_accessed=2 * exp_size * width * (units + rows),
        ),
        compiler_params=pltpu.CompilerParams(vmem_limit_bytes=VMEM_LIMIT),
        name="expert_out",
    )(idx, act, w_down)


def masks(size):
    return [1 << i for i in range(size.bit_length() - 1)]


def bit_orders(ctx_size, exp_size):
    low = [("ctx", m) for m in masks(ctx_size)]
    across = [("exp", m) for m in masks(exp_size)[1:]][::-1]
    cut = max(1, len(low) // 3)
    return [
        low[::-1] + across,
        across + low[::-1],
        low[:cut][::-1] + across + low[cut:][::-1],
    ]


def spread(value, order, core_bit):
    have = value
    for bit in order[:-1]:
        have = jnp.stack([have, swap(have, bit)])
    if len(order) == 1:
        have = value
    halves = [have, swap(have, order[-1])]
    return [part for half in halves for part in (half, swap(half, core_bit))]


def gather_sum(parts, order, core_bit):
    kept0, kept1, sent0, sent1 = parts
    came1 = swap(sent1, core_bit)
    leaving = (kept1.astype(f32) + came1.astype(f32)).astype(bf16)
    came = swap(leaving, order[0])
    came0 = swap(sent0, core_bit)
    total = kept0.astype(f32) + came0.astype(f32) + came.astype(f32)
    for bit in order[1:]:
        total = total[0] + swap(total[1].astype(bf16), bit).astype(f32)
    return total


def per_device(
    residual,
    query_rows,
    key_rows,
    value_rows,
    log_decay,
    norm_gain,
    expert_ids,
    gate_weights,
    w_gate,
    w_up,
    w_down,
):
    count, columns = residual.shape
    heads = columns // HEAD
    ctx_size, exp_size = lax.axis_size("ctx"), lax.axis_size("exp")
    ctx_me, exp_me = lax.axis_index("ctx"), lax.axis_index("exp")
    core_bit = ("exp", 1)
    orders = bit_orders(ctx_size, exp_size)
    chunks = len(orders)
    per = heads // chunks
    width = per * HEAD

    inside, cumul, local, *sends = local_parts(query_rows, key_rows, value_rows, log_decay, per)

    decays = jnp.pad(jnp.sum(log_decay, axis=0), (0, count - heads))
    facts = jnp.concatenate(
        [expert_ids.T.astype(f32), gate_weights.T, decays[None], jnp.zeros((3, count), f32)], axis=0
    )[None]
    states = [None] * chunks
    totals = [local[c * per : (c + 1) * per] for c in range(chunks)]
    mine = facts[0, 4, :heads]
    before = jnp.zeros((heads,), f32)
    ctx_masks = masks(ctx_size)
    for mask in ctx_masks:
        bit = ("ctx", mask)
        came = swap(facts, bit)
        theirs = jnp.sum(came[:, 4, :heads], axis=0)
        facts = jnp.concatenate([facts, came], axis=0)
        later = (ctx_me & mask) != 0
        weight = jnp.where(later, jnp.exp(before), 0.0)
        fade = jnp.exp(jnp.where(later, mine, theirs))
        for c in range(chunks):
            other = swap(sends[c], bit).astype(f32)
            head = slice(c * per, (c + 1) * per)
            gained = weight[head][:, None, None] * other
            states[c] = gained if states[c] is None else states[c] + gained
            if mask != ctx_masks[-1]:
                scaled = fade[head][:, None, None] * jnp.where(later, other, totals[c])
                totals[c] = scaled + jnp.where(later, totals[c], other)
                sends[c] = totals[c].astype(bf16)
        before = before + jnp.where(later, theirs, 0.0)
        mine = mine + theirs
    matches = (facts[:, 0:2, :] == exp_me.astype(f32)).astype(f32)
    scale = jnp.sum(matches * facts[:, 2:4, :], axis=1)

    gain = norm_gain[None]
    relative = jnp.arange(exp_size, dtype=jnp.int32)
    hidden, gathered = [], []
    for c in range(chunks):
        rows = hidden_rows(c, per, query_rows, inside, residual, gain, cumul, states[c].astype(bf16))
        hidden.append(rows)
        gathered.append(spread(rows, orders[c], core_bit))
    total = None
    for c in range(chunks):
        order = orders[c]
        total = expert_in(
            gathered[c], order[:-1][::-1], order[-1], core_bit,
            (exp_me ^ relative) * chunks + c, w_gate[0], w_up[0],
            total, scale if c == chunks - 1 else None, ctx_size, exp_size,
        )
    steps = [r for r in range(exp_size) if r & 1] + [r for r in range(exp_size) if not r & 1]
    mixed = []
    for c in range(chunks):
        order = orders[c]
        idx = (exp_me ^ jnp.array(steps, jnp.int32)) * chunks + c
        parts = expert_out(
            total, w_down[0], idx, steps, order[:-1][::-1], order[-1], core_bit, ctx_size, width
        )
        added = gather_sum(parts, order[::-1], core_bit)
        mixed.append((hidden[c].astype(f32) + added).astype(bf16))
    return jnp.concatenate(mixed, axis=1)


def solution(mesh):
    return jax.shard_map(
        per_device,
        mesh=mesh,
        in_specs=(
            P("ctx", "exp"),
            P("ctx", "exp"),
            P("ctx", "exp"),
            P("ctx", "exp"),
            P("ctx", "exp"),
            P("exp"),
            P("ctx", None),
            P("ctx", None),
            P("exp", None, "ctx"),
            P("exp", None, "ctx"),
            P("exp", "ctx", None),
        ),
        out_specs=P("ctx", "exp"),
        check_vma=False,
    )
```
